128 devices in a mesh: blk: 16 (over z_lo, x, core), narrow: 8 (over z_hi, y).
Axes of the slice: x: 4, y: 4, z: 4 (z_hi: 2, z_lo: 2; z = z_hi * 2 + z_lo), core: 2. Of those that a mesh axis runs over, the one named last changes fastest.
Arguments:
- codes: bfloat16 [24576, 12288], P(('blk', 'narrow')), may hold values from -24 to 24
- signals: bfloat16 [24576, 192], P(('blk', 'narrow')), may hold values from -6 to 6
- dictionary: bfloat16 [12288, 192], P('blk'), may hold values from -0.0546875 to 0.0546875
Outputs:
- new_codes: bfloat16 [24576, 12288], P(('blk', 'narrow'))
- dict_grad: float32 [12288, 192], P(('blk', 'narrow'))
The draws below stay inside these ranges and needn't reach their ends.
All inputs are finite; a program needn't handle non-finite values.
Results may differ from the reference program's by a relative error of at most 0.0095.
Values may be sent and summed in bfloat16 or wider, within the bound.
No kernel may reach another device: no remote copies, remote signals or barrier semaphores. Data moves between devices by JAX's collectives and lax.ppermute only.
A program may use at most 64 MiB of HBM per device.

```python
import jax
import jax.numpy as jnp
from jax import lax

F = 192
K = 12288
NB = 24576
N_BLK = 16


def raised(array, own_key, source, target, shards_of, factor):
    owner, partner = [(jnp.arange(array.shape[axis_at]) // (array.shape[axis_at] // shards_of)).reshape([-1 if axis == axis_at else 1 for axis in range(array.ndim)]) for axis_at in (source, target)]
    chosen = jax.random.permutation(own_key, shards_of)[partner]
    strong = (owner == chosen) | (owner == (partner + shards_of // 2) % shards_of)
    return jnp.where(strong, factor * array, array)


def shard_levels(key, dims, cuts, least, largest):
    def one(dim, shards_of):
        draws = jax.random.uniform(jax.random.fold_in(jax.random.fold_in(key, 6), dim), (shards_of,), jnp.float32, least / len(cuts), largest / len(cuts))
        return jnp.repeat(jnp.exp(draws), dims[dim] // shards_of).reshape((-1,) + (1,) * (len(dims) - dim - 1))

    factor_of = one(*cuts[0])
    for cut in cuts[1:]:
        factor_of = factor_of * one(*cut)
    return factor_of


def centred(own_key, shape, deviation, reach, split=(), dtype=jnp.bfloat16):
    gain = shard_levels(own_key, shape, split, -0.22, 0.18) if split else 1.0
    result = jax.random.normal(own_key, shape, jnp.float32) * deviation * gain
    return jnp.minimum(jnp.maximum(result, -reach), reach).astype(dtype)


def noise_with(own_key, dims, width, reach, split, heavy, kind=jnp.bfloat16):
    drawn = width * jax.random.normal(own_key, dims, jnp.float32)
    if split:
        drawn = drawn * shard_levels(own_key, dims, split, -0.22, 0.18)
    return jnp.clip(raised(drawn, jax.random.fold_in(own_key, 3), *heavy), -reach, reach).astype(kind)


def setup_inputs(seed: int = 0) -> dict:
    seeds = jax.random.split(jax.random.key(seed), 4)
    return {
        "codes": noise_with(seeds[0], (NB, K), 1.0, 24.0, ((0, 128),), (0, 1, 128, 5.5)),
        "signals": centred(seeds[1], (NB, F), 1.0, 6.0, ((0, 128),)),
        "dictionary": centred(seeds[2], (K, F), K ** -0.5, 0.0546875, ((0, 16),)),
    }


def shrink(values):
    return jnp.sign(values) * jnp.maximum(jnp.abs(values) - 0.5, 0.0)


def reference(codes, signals, dictionary):
    total_rows = codes.shape[0]
    block_rows = total_rows // N_BLK
    block_count = N_BLK
    code_blocks = codes.reshape(block_count, block_rows, codes.shape[1])
    signal_blocks = signals.reshape(block_count, block_rows, signals.shape[1])

    def one_block(pair):
        code_part, signal_part = pair
        estimate = jnp.dot(code_part, dictionary, preferred_element_type=jnp.float32)
        misfit = (estimate - signal_part.astype(jnp.float32)).astype(jnp.bfloat16)
        correlation = lax.dot_general(misfit, dictionary, (((1,), (1,)), ((), ())), preferred_element_type=jnp.float32)
        fresh = shrink(code_part.astype(jnp.float32) - 4.0 * correlation).astype(jnp.bfloat16)
        second = jnp.dot(fresh, dictionary, preferred_element_type=jnp.float32)
        misfit_two = (second - signal_part.astype(jnp.float32)).astype(jnp.bfloat16)
        return fresh, misfit_two

    fresh_blocks, misfit_blocks = lax.map(one_block, (code_blocks, signal_blocks))
    new_codes = fresh_blocks.reshape(total_rows, codes.shape[1])
    misfit_two = misfit_blocks.reshape(total_rows, signals.shape[1])
    dict_grad = lax.dot_general(new_codes, misfit_two, (((0,), (0,)), ((), ())), preferred_element_type=jnp.float32)
    return new_codes, dict_grad * (float(total_rows) ** -0.5)
```

```python
import functools

import jax
import jax.numpy as jnp
from jax import lax
from jax.experimental import pallas as pl
from jax.experimental.pallas import tpu as pltpu
from jax.sharding import Mesh
from jax.sharding import PartitionSpec as P


AXES = ("z_lo", "x", "core", "z_hi", "y")
SIZES = (2, 4, 2, 2, 4)
ANY = pl.BlockSpec(memory_space=pl.ANY)
SMEM = pl.BlockSpec(memory_space=pltpu.SMEM)
VMEM = pl.BlockSpec(memory_space=pltpu.VMEM)
F32, BF16 = jnp.float32, jnp.bfloat16


def z_step(step):
    def place(z):
        return (z % 2) * 2 + z // 2

    return [(place(z), place((z + step) % 4)) for z in range(4)]


def send_x(value, step):
    return lax.ppermute(value, "x", [(i, (i + step) % 4) for i in range(4)])


def send_z(value, step):
    return lax.ppermute(value, ("z_lo", "z_hi"), z_step(step))


def send_core(value):
    return lax.ppermute(value, "core", [(0, 1), (1, 0)])


def columns(block, width):
    return pl.ds(pl.multiple_of(block * width, 128), width)


def split_kernel(where, codes, own, away, sems):
    width = own.shape[1] // 8
    core = where[0]
    copies = []
    for q in range(8):
        for side, (target, half) in enumerate(((away, 1 - core), (own, core))):
            copies.append(
                pltpu.make_async_copy(
                    codes.at[:, columns(2 * q + half, width)],
                    target.at[:, columns(q, width)],
                    sems.at[side, q],
                )
            )
    for copy in copies:
        copy.start()
    for copy in copies:
        copy.wait()


def load_chunks(place, own, other, parts, codes_buf, atoms_buf, sems):
    rows, width = own.shape[0], atoms_buf.shape[2]
    groups = []
    for k, pieces in enumerate(parts):
        group = []
        span = columns(place[k], width)
        group.append(pltpu.make_async_copy(own.at[:, span], codes_buf.at[k, 0:rows], sems.at[k, 0]))
        group.append(pltpu.make_async_copy(other.at[:, span], codes_buf.at[k, rows : 2 * rows], sems.at[k, 1]))
        at = 0
        for s, piece in enumerate(pieces):
            high = piece.shape[0]
            group.append(pltpu.make_async_copy(piece, atoms_buf.at[k, at : at + high], sems.at[k, 2 + s]))
            at += high
        groups.append(group)
    return groups


def along_atoms(left, right):
    return lax.dot_general(left, right, (((1,), (1,)), ((), ())), preferred_element_type=F32)


def estimate_kernel(counts, has_start, *refs):
    place, own, other = refs[:3]
    at = 3
    start = None
    if has_start:
        start = refs[at]
        at += 1
    parts = []
    for count in counts:
        parts.append(refs[at : at + count])
        at += count
    out, codes_buf, atoms_buf, sems = refs[at:]
    groups = load_chunks(place, own, other, parts, codes_buf, atoms_buf, sems)
    for group in groups:
        for copy in group:
            copy.start()
    total = start[...] if has_start else None
    for k, group in enumerate(groups):
        for copy in group:
            copy.wait()
        term = along_atoms(codes_buf[k], atoms_buf[k])
        total = term if total is None else total + term
    out[...] = total


def estimate(place, own, other, start, parts):
    rows, width = own.shape[0], parts[0][0].shape[1]
    features = sum(p.shape[0] for p in parts[0])
    counts = tuple(len(p) for p in parts)
    flat = [p for pieces in parts for p in pieces]
    given = [place, own, other] + ([] if start is None else [start]) + flat
    specs = [SMEM, ANY, ANY] + ([] if start is None else [VMEM]) + [ANY] * len(flat)
    n = len(parts)
    return pl.pallas_call(
        functools.partial(estimate_kernel, counts, start is not None),
        out_shape=jax.ShapeDtypeStruct((2 * rows, features), F32),
        in_specs=specs,
        out_specs=VMEM,
        scratch_shapes=[
            pltpu.VMEM((n, 2 * rows, width), BF16),
            pltpu.VMEM((n, features, width), BF16),
            pltpu.SemaphoreType.DMA((n, 4)),
        ],
        name="estimate",
    )(*given)


def update_kernel(counts, *refs):
    place, own, other, mine, theirs, signal_own, signal_other = refs[:7]
    at = 7
    parts = []
    for count in counts:
        parts.append(refs[at : at + count])
        at += count
    fresh_own, fresh_other, second, codes_buf, atoms_buf, sems, out_sems = refs[at:]
    rows, width = own.shape[0], atoms_buf.shape[2]
    groups = load_chunks(place, own, other, parts, codes_buf, atoms_buf, sems)
    for group in groups:
        for copy in group:
            copy.start()
    signal = jnp.concatenate([signal_own[...], signal_other[...]], axis=0).astype(F32)
    misfit = (mine[...] + theirs[...] - signal).astype(BF16)
    total = None
    outs = []
    for k, group in enumerate(groups):
        for copy in group:
            copy.wait()
        atoms = atoms_buf[k]
        correlation = jnp.dot(misfit, atoms, preferred_element_type=F32)
        value = codes_buf[k].astype(F32) - 4.0 * correlation
        fresh = (value - jnp.clip(value, -0.5, 0.5)).astype(BF16)
        codes_buf[k] = fresh
        span = columns(place[k], width)
        for s, (target, low) in enumerate(((fresh_own, 0), (fresh_other, rows))):
            copy = pltpu.make_async_copy(codes_buf.at[k, low : low + rows], target.at[:, span], out_sems.at[k, s])
            copy.start()
            outs.append(copy)
        term = along_atoms(fresh, atoms)
        total = term if total is None else total + term
    second[...] = total
    for copy in outs:
        copy.wait()


def update(place, own, other, mine, theirs, signal_own, signal_other, parts):
    rows, width = own.shape[0], parts[0][0].shape[1]
    features = sum(p.shape[0] for p in parts[0])
    counts = tuple(len(p) for p in parts)
    flat = [p for pieces in parts for p in pieces]
    n = len(parts)
    return pl.pallas_call(
        functools.partial(update_kernel, counts),
        out_shape=(
            jax.ShapeDtypeStruct(own.shape, BF16),
            jax.ShapeDtypeStruct(own.shape, BF16),
            jax.ShapeDtypeStruct((2 * rows, features), F32),
        ),
        in_specs=[SMEM, ANY, ANY] + [VMEM] * 4 + [ANY] * len(flat),
        out_specs=(ANY, ANY, VMEM),
        scratch_shapes=[
            pltpu.VMEM((n, 2 * rows, width), BF16),
            pltpu.VMEM((n, features, width), BF16),
            pltpu.SemaphoreType.DMA((n, 4)),
            pltpu.SemaphoreType.DMA((n, 2)),
        ],
        name="update",
    )(place, own, other, mine, theirs, signal_own, signal_other, *flat)


def gradient_kernel(mine, theirs, signal_own, signal_other, own, other, out, buf, sems):
    rows, width = own.shape[0], buf.shape[2]
    groups = []
    for q in range(8):
        span = columns(q, width)
        pair = (
            pltpu.make_async_copy(own.at[:, span], buf.at[q, 0:rows], sems.at[q, 0]),
            pltpu.make_async_copy(other.at[:, span], buf.at[q, rows : 2 * rows], sems.at[q, 1]),
        )
        for copy in pair:
            copy.start()
        groups.append(pair)
    signal = jnp.concatenate([signal_own[...], signal_other[...]], axis=0).astype(F32)
    misfit = (mine[...] + theirs[...] - signal).astype(BF16)
    wide = jnp.concatenate([misfit, misfit[:, 128:192]], axis=1)
    part = width // 8
    low = lax.broadcasted_iota(jnp.int32, (part // 2, 128), 1) < 64
    for q in range(8):
        for copy in groups[q]:
            copy.wait()
        product = lax.dot_general(buf[q], wide, (((0,), (0,)), ((), ())), preferred_element_type=F32)
        for n in range(8):
            piece = product[n * part : (n + 1) * part]
            out[q * 8 + n, 0:part] = piece[:, 0:128].astype(BF16)
            tail = jnp.where(low, piece[: part // 2, 128:256], piece[part // 2 :, 128:256])
            out[q * 8 + n, part : part + part // 2] = tail.astype(BF16)


def gradient(mine, theirs, signal_own, signal_other, own, other):
    rows, width = own.shape[0], own.shape[1] // 8
    part = width // 8
    return pl.pallas_call(
        gradient_kernel,
        out_shape=jax.ShapeDtypeStruct((64, part + part // 2, 128), BF16),
        in_specs=[VMEM] * 4 + [ANY, ANY],
        out_specs=VMEM,
        scratch_shapes=[
            pltpu.VMEM((8, 2 * rows, width), BF16),
            pltpu.SemaphoreType.DMA((8, 2)),
        ],
        name="gradient",
    )(mine, theirs, signal_own, signal_other, own, other)


def finish_kernel(scale, where, pieces, fresh_own, fresh_back, codes_out, grad_out, sems):
    width = fresh_own.shape[1] // 8
    core = where[0]
    copies = []
    for q in range(8):
        for side, (source, half) in enumerate(((fresh_own, core), (fresh_back, 1 - core))):
            copies.append(
                pltpu.make_async_copy(
                    source.at[:, columns(q, width)],
                    codes_out.at[:, columns(2 * q + half, width)],
                    sems.at[side, q],
                )
            )
    for copy in copies:
        copy.start()
    total = pieces[0].astype(F32)
    for i in range(1, pieces.shape[0]):
        total = total + pieces[i].astype(F32)
    total = total * scale
    part = grad_out.shape[0]
    grad_out[:, 0:128] = total[0:part]
    grad_out[0 : part // 2, 128:192] = total[part:, 0:64]
    grad_out[part // 2 :, 128:192] = total[part:, 64:128]
    for copy in copies:
        copy.wait()


def body(codes, signals, dictionary):
    rows, atom_count = codes.shape
    core = lax.axis_index("core").astype(jnp.int32).reshape(1)
    x, z_lo = lax.axis_index("x"), lax.axis_index("z_lo")
    half = jax.ShapeDtypeStruct((rows, atom_count // 2), BF16)
    own, away = pl.pallas_call(
        split_kernel,
        out_shape=(half, half),
        in_specs=[SMEM, ANY],
        out_specs=(ANY, ANY),
        scratch_shapes=[pltpu.SemaphoreType.DMA((2, 8))],
        name="split",
    )(core, codes)
    other = send_core(away)
    signal_other = send_core(signals)

    atoms = dictionary.T
    mid = atoms.shape[0] // 2
    left, right = send_x(atoms, 1), send_x(atoms, -1)
    near = (send_z(atoms[:mid], 1), send_z(atoms[mid:], -1))
    near_left, near_right = send_z(left, 1), send_z(right, -1)
    far = (send_x(left[:mid], 1), send_x(right[mid:], -1))
    near_far = (send_z(far[0], 1), send_z(far[1], -1))

    def at(dz, dx):
        return ((z_lo + dz) % 2) * 4 + (x + dx) % 4

    plan = [
        (at(0, 0), (atoms,)),
        (at(0, 3), (left,)),
        (at(0, 1), (right,)),
        (at(1, 0), near),
        (at(1, 3), (near_left,)),
        (at(1, 1), (near_right,)),
        (at(0, 2), far),
        (at(1, 2), near_far),
    ]
    place = jnp.stack([p[0] for p in plan]).astype(jnp.int32)
    parts = [p[1] for p in plan]
    mine = None
    for low, high in ((0, 3), (3, 6), (6, 8)):
        mine = estimate(place[low:high], own, other, mine, parts[low:high])
    theirs = send_core(mine)
    theirs = jnp.concatenate([theirs[rows:], theirs[:rows]], axis=0)
    fresh_own, fresh_other, second = update(place, own, other, mine, theirs, signals, signal_other, parts)
    second_theirs = send_core(second)
    second_theirs = jnp.concatenate([second_theirs[rows:], second_theirs[:rows]], axis=0)
    fresh_back = send_core(fresh_other)
    pieces = gradient(second, second_theirs, signals, signal_other, fresh_own, fresh_other)
    pieces = lax.all_to_all(pieces, ("z_lo", "x", "z_hi", "y"), 0, 0, tiled=True)
    total_rows = rows
    for size in SIZES:
        total_rows *= size
    part = atom_count // 128
    return pl.pallas_call(
        functools.partial(finish_kernel, float(total_rows) ** -0.5),
        out_shape=(
            jax.ShapeDtypeStruct(codes.shape, BF16),
            jax.ShapeDtypeStruct((part, signals.shape[1]), F32),
        ),
        in_specs=[SMEM, VMEM, ANY, ANY],
        out_specs=(ANY, VMEM),
        scratch_shapes=[pltpu.SemaphoreType.DMA((2, 8))],
        name="finish",
    )(core, pieces, fresh_own, fresh_back)


def solution(mesh):
    fine = Mesh(mesh.devices.reshape(SIZES), AXES)
    every = P(AXES, None)
    return jax.shard_map(
        body,
        mesh=fine,
        in_specs=(every, every, P(("z_lo", "x", "core"), None)),
        out_specs=(every, every),
        check_vma=False,
    )
```

```python
import functools

import jax
import jax.numpy as jnp
from jax import lax
from jax.experimental import pallas as pl
from jax.experimental.pallas import tpu as pltpu
from jax.sharding import Mesh
from jax.sharding import PartitionSpec as P


AXES = ("z_lo", "x", "core", "z_hi", "y")
SIZES = (2, 4, 2, 2, 4)
ANY = pl.BlockSpec(memory_space=pl.ANY)
SMEM = pl.BlockSpec(memory_space=pltpu.SMEM)
VMEM = pl.BlockSpec(memory_space=pltpu.VMEM)
F32, BF16 = jnp.float32, jnp.bfloat16
PARAMS = pltpu.CompilerParams(vmem_limit_bytes=24 << 20)


def near_memory(value):
    return pltpu.with_memory_space_constraint(value, pltpu.VMEM)


def z_step(step):
    def place(z):
        return (z % 2) * 2 + z // 2

    return [(place(z), place((z + step) % 4)) for z in range(4)]


def send_x(value, step):
    return lax.ppermute(value, "x", [(i, (i + step) % 4) for i in range(4)])


def send_z(value, step):
    return lax.ppermute(value, ("z_lo", "z_hi"), z_step(step))


def send_core(value):
    return lax.ppermute(value, "core", [(0, 1), (1, 0)])


def columns(block, width):
    return pl.ds(pl.multiple_of(block * width, 128), width)


def chunk_place(shift, x, z_lo):
    dz, dx = shift
    return ((z_lo[0] + dz) % 2) * 4 + (x[0] + dx) % 4


def split_kernel(core, codes, atoms, own, away, low, high, sems):
    width = own.shape[1] // 8
    mid = low.shape[0]
    copies = []
    for side, (target, half) in enumerate(((away, 1 - core[0]), (own, core[0]))):
        for q in range(8):
            copies.append(
                pltpu.make_async_copy(
                    codes.at[:, columns(2 * q + half, width)],
                    target.at[:, columns(q, width)],
                    sems.at[side, q],
                )
            )
    copies.append(pltpu.make_async_copy(atoms.at[0:mid], low, sems.at[2, 0]))
    copies.append(pltpu.make_async_copy(atoms.at[mid : 2 * mid], high, sems.at[2, 1]))
    for copy in copies:
        copy.start()
    for copy in copies:
        copy.wait()


def split(core, codes, atoms):
    rows, atom_count = codes.shape
    half = pltpu.VMEM((rows, atom_count // 2), BF16)
    piece = pltpu.VMEM((atoms.shape[0] // 2, atoms.shape[1]), BF16)
    return pl.pallas_call(
        split_kernel,
        out_shape=(half, half, piece, piece),
        in_specs=[SMEM, ANY, ANY],
        out_specs=(VMEM,) * 4,
        scratch_shapes=[pltpu.SemaphoreType.DMA((3, 8))],
        compiler_params=PARAMS,
        name="split",
    )(core, codes, atoms)


def along_atoms(left, right):
    return lax.dot_general(left, right, (((1,), (1,)), ((), ())), preferred_element_type=F32)


def whole(pieces):
    values = [piece[...] for piece in pieces]
    return values[0] if len(values) == 1 else jnp.concatenate(values, axis=0)


def take(refs, counts):
    parts, at = [], 0
    for count in counts:
        parts.append(refs[at : at + count])
        at += count
    return parts, refs[at:]


def estimate_kernel(shifts, counts, has_start, x, z_lo, own, other, *refs):
    start = refs[0] if has_start else None
    parts, rest = take(refs[1:] if has_start else refs, counts)
    (out,) = rest
    rows = own.shape[0]
    width = own.shape[1] // 8
    for k, pieces in enumerate(parts):
        atoms = whole(pieces)
        span = columns(chunk_place(shifts[k], x, z_lo), width)
        for low, source in ((0, own), (rows, other)):
            term = along_atoms(source[:, span], atoms)
            if k:
                out[low : low + rows] += term
            elif has_start:
                out[low : low + rows] = start[low : low + rows] + term
            else:
                out[low : low + rows] = term


def estimate(x, z_lo, own, other, start, shifts, parts):
    rows = own.shape[0]
    features = sum(p.shape[0] for p in parts[0])
    counts = tuple(len(p) for p in parts)
    flat = [p for pieces in parts for p in pieces]
    given = [own, other] + ([] if start is None else [start]) + flat
    return pl.pallas_call(
        functools.partial(estimate_kernel, shifts, counts, start is not None),
        out_shape=pltpu.VMEM((2 * rows, features), F32),
        in_specs=[SMEM, SMEM] + [VMEM] * len(given),
        out_specs=VMEM,
        compiler_params=PARAMS,
        name="estimate",
    )(x, z_lo, *[near_memory(v) for v in given])


def misfit_of(mine, theirs, signal_own, signal_other):
    rows = signal_own.shape[0]
    first = mine[0:rows] + theirs[rows : 2 * rows] - signal_own[...].astype(F32)
    second = mine[rows : 2 * rows] + theirs[0:rows] - signal_other[...].astype(F32)
    return jnp.concatenate([first.astype(BF16), second.astype(BF16)], axis=0)


def update_kernel(shifts, counts, x, z_lo, own, other, mine, theirs, signal_own, signal_other, *refs):
    parts, rest = take(refs, counts)
    fresh_own, fresh_other, out = rest
    rows = own.shape[0]
    width = own.shape[1] // 8
    misfit = misfit_of(mine, theirs, signal_own, signal_other)
    for k, pieces in enumerate(parts):
        atoms = whole(pieces)
        span = columns(chunk_place(shifts[k], x, z_lo), width)
        for low, source, target in ((0, own, fresh_own), (rows, other, fresh_other)):
            correlation = jnp.dot(misfit[low : low + rows], atoms, preferred_element_type=F32)
            value = source[:, span].astype(F32) - 4.0 * correlation
            fresh = (value - jnp.clip(value, -0.5, 0.5)).astype(BF16)
            target[:, span] = fresh
            term = along_atoms(fresh, atoms)
            if k:
                out[low : low + rows] += term
            else:
                out[low : low + rows] = term


def update(x, z_lo, own, other, mine, theirs, signal_own, signal_other, shifts, parts):
    rows = own.shape[0]
    features = sum(p.shape[0] for p in parts[0])
    counts = tuple(len(p) for p in parts)
    flat = [p for pieces in parts for p in pieces]
    given = [own, other, mine, theirs, signal_own, signal_other] + flat
    return pl.pallas_call(
        functools.partial(update_kernel, shifts, counts),
        out_shape=(
            pltpu.VMEM(own.shape, BF16),
            pltpu.VMEM(own.shape, BF16),
            pltpu.VMEM((2 * rows, features), F32),
        ),
        in_specs=[SMEM, SMEM] + [VMEM] * len(given),
        out_specs=(VMEM,) * 3,
        compiler_params=PARAMS,
        name="update",
    )(x, z_lo, *[near_memory(v) for v in given])


def gradient_kernel(mine, theirs, signal_own, signal_other, own, other, out):
    rows = own.shape[0]
    width = own.shape[1] // 8
    misfit = misfit_of(mine, theirs, signal_own, signal_other)
    wide = jnp.concatenate([misfit, misfit[:, 128:192]], axis=1)
    part = width // 8
    low = lax.broadcasted_iota(jnp.int32, (part // 2, 128), 1) < 64
    for q in range(8):
        span = slice(q * width, (q + 1) * width)
        codes = jnp.concatenate([own[:, span], other[:, span]], axis=0)
        product = lax.dot_general(codes, wide, (((0,), (0,)), ((), ())), preferred_element_type=F32)
        for n in range(8):
            piece = product[n * part : (n + 1) * part]
            out[q * 8 + n, 0:part] = piece[:, 0:128].astype(BF16)
            tail = jnp.where(low, piece[: part // 2, 128:256], piece[part // 2 :, 128:256])
            out[q * 8 + n, part : part + part // 2] = tail.astype(BF16)


def gradient(mine, theirs, signal_own, signal_other, own, other):
    part = own.shape[1] // 64
    given = [mine, theirs, signal_own, signal_other, own, other]
    return pl.pallas_call(
        gradient_kernel,
        out_shape=pltpu.VMEM((64, part + part // 2, 128), BF16),
        in_specs=[VMEM] * 6,
        out_specs=VMEM,
        compiler_params=PARAMS,
        name="gradient",
    )(*[near_memory(v) for v in given])


def finish_kernel(scale, core, pieces, fresh_own, fresh_back, codes_out, grad_out, sems):
    width = fresh_own.shape[1] // 8
    copies = []
    for side, (source, half) in enumerate(((fresh_own, core[0]), (fresh_back, 1 - core[0]))):
        for q in range(8):
            copies.append(
                pltpu.make_async_copy(
                    source.at[:, columns(q, width)],
                    codes_out.at[:, columns(2 * q + half, width)],
                    sems.at[side, q],
                )
            )
    for copy in copies:
        copy.start()
    part = grad_out.shape[0]
    total = pieces[0].astype(F32)
    for i in range(1, pieces.shape[0]):
        total = total + pieces[i].astype(F32)
    total = total * scale
    grad_out[:, 0:128] = total[0:part]
    grad_out[0 : part // 2, 128:192] = total[part:, 0:64]
    grad_out[part // 2 :, 128:192] = total[part:, 64:128]
    for copy in copies:
        copy.wait()


def finish(scale, core, pieces, fresh_own, fresh_back, codes_shape, grad_shape):
    given = [pieces, fresh_own, fresh_back]
    return pl.pallas_call(
        functools.partial(finish_kernel, scale),
        out_shape=(jax.ShapeDtypeStruct(codes_shape, BF16), jax.ShapeDtypeStruct(grad_shape, F32)),
        in_specs=[SMEM] + [VMEM] * 3,
        out_specs=(ANY, VMEM),
        scratch_shapes=[pltpu.SemaphoreType.DMA((2, 8))],
        compiler_params=PARAMS,
        name="finish",
    )(core, *[near_memory(v) for v in given])


def body(codes, signals, dictionary):
    rows, atom_count = codes.shape
    core, x, z_lo = (lax.axis_index(a).astype(jnp.int32).reshape(1) for a in ("core", "x", "z_lo"))
    atoms = dictionary.T
    mid = atoms.shape[0] // 2
    own, away, low, high = split(core, codes, atoms)
    other = send_core(away)
    signal_other = send_core(signals)

    left, right = send_x(atoms, 1), send_x(atoms, -1)
    near = (send_z(low, 1), send_z(high, -1))
    near_left, near_right = send_z(left, 1), send_z(right, -1)
    far = (send_x(left[:mid], 1), send_x(right[mid:], -1))
    near_far = (send_z(far[0], 1), send_z(far[1], -1))
    plan = [
        ((0, 0), (low, high)),
        ((0, 3), (left,)),
        ((0, 1), (right,)),
        ((1, 0), near),
        ((1, 3), (near_left,)),
        ((1, 1), (near_right,)),
        ((0, 2), far),
        ((1, 2), near_far),
    ]
    shifts = [p[0] for p in plan]
    parts = [p[1] for p in plan]
    mine = None
    for first, last in ((0, 3), (3, 6), (6, 8)):
        mine = estimate(x, z_lo, own, other, mine, shifts[first:last], parts[first:last])
    theirs = send_core(mine)
    fresh_own, fresh_other, second = update(
        x, z_lo, own, other, mine, theirs, signals, signal_other, shifts, parts
    )
    second_theirs = send_core(second)
    fresh_back = send_core(fresh_other)
    pieces = gradient(second, second_theirs, signals, signal_other, fresh_own, fresh_other)
    pieces = lax.all_to_all(pieces, ("z_lo", "x", "z_hi", "y"), 0, 0, tiled=True)
    total_rows = rows
    for size in SIZES:
        total_rows *= size
    grad_shape = (atom_count // 128, signals.shape[1])
    return finish(float(total_rows) ** -0.5, core, pieces, fresh_own, fresh_back, codes.shape, grad_shape)


def solution(mesh):
    fine = Mesh(mesh.devices.reshape(SIZES), AXES)
    every = P(AXES, None)
    return jax.shard_map(
        body,
        mesh=fine,
        in_specs=(every, every, P(("z_lo", "x", "core"), None)),
        out_specs=(every, every),
        check_vma=False,
    )
```

```python
import functools

import jax
import jax.numpy as jnp
from jax import lax
from jax.experimental import pallas as pl
from jax.experimental.pallas import tpu as pltpu
from jax.sharding import Mesh
from jax.sharding import PartitionSpec as P


AXES = ("z_lo", "x", "core", "z_hi", "y")
SIZES = (2, 4, 2, 2, 4)
ANY = pl.BlockSpec(memory_space=pl.ANY)
SMEM = pl.BlockSpec(memory_space=pltpu.SMEM)
VMEM = pl.BlockSpec(memory_space=pltpu.VMEM)
F32, BF16 = jnp.float32, jnp.bfloat16
PARAMS = pltpu.CompilerParams(vmem_limit_bytes=24 << 20)


def near_memory(value):
    return pltpu.with_memory_space_constraint(value, pltpu.VMEM)


def far_memory(value):
    return pltpu.with_memory_space_constraint(value, pltpu.HBM)


def z_step(step):
    def place(z):
        return (z % 2) * 2 + z // 2

    return [(place(z), place((z + step) % 4)) for z in range(4)]


def send_x(value, step):
    return lax.ppermute(value, "x", [(i, (i + step) % 4) for i in range(4)])


def send_z(value, step):
    return lax.ppermute(value, ("z_lo", "z_hi"), z_step(step))


def send_core(value):
    return lax.ppermute(value, "core", [(0, 1), (1, 0)])


def columns(block, width):
    return pl.ds(pl.multiple_of(block * width, 128), width)


def chunk_place(shift, x, z_lo):
    dz, dx = shift
    return ((z_lo[0] + dz) % 2) * 4 + (x[0] + dx) % 4


def halve_kernel(core, x, z_lo, atoms, low, high, sems):
    mid = low.shape[0]
    copies = [
        pltpu.make_async_copy(atoms.at[0:mid], low, sems.at[0]),
        pltpu.make_async_copy(atoms.at[mid : 2 * mid], high, sems.at[1]),
    ]
    for copy in copies:
        copy.start()
    for copy in copies:
        copy.wait()


def halve(core, x, z_lo, atoms):
    piece = pltpu.VMEM((atoms.shape[0] // 2, atoms.shape[1]), BF16)
    return pl.pallas_call(
        halve_kernel,
        out_shape=(piece, piece),
        in_specs=[SMEM, SMEM, SMEM, ANY],
        out_specs=(VMEM, VMEM),
        scratch_shapes=[pltpu.SemaphoreType.DMA((2,))],
        compiler_params=PARAMS,
        name="halve",
    )(core, x, z_lo, far_memory(atoms))


def split_kernel(core, codes, own, away, sems):
    width = own.shape[1] // 8
    copies = []
    for side, (target, half) in enumerate(((away, 1 - core[0]), (own, core[0]))):
        for q in range(8):
            copies.append(
                pltpu.make_async_copy(
                    codes.at[:, columns(2 * q + half, width)],
                    target.at[:, columns(q, width)],
                    sems.at[side, q],
                )
            )
    for copy in copies:
        copy.start()
    for copy in copies:
        copy.wait()


def split(core, codes):
    rows, atom_count = codes.shape
    half = pltpu.VMEM((rows, atom_count // 2), BF16)
    return pl.pallas_call(
        split_kernel,
        out_shape=(half, half),
        in_specs=[SMEM, ANY],
        out_specs=(VMEM, VMEM),
        scratch_shapes=[pltpu.SemaphoreType.DMA((2, 8))],
        compiler_params=PARAMS,
        name="split",
    )(core, far_memory(codes))


def along_atoms(left, right):
    return lax.dot_general(left, right, (((1,), (1,)), ((), ())), preferred_element_type=F32)


def whole(pieces):
    values = [piece[...] for piece in pieces]
    return values[0] if len(values) == 1 else jnp.concatenate(values, axis=0)


def take(refs, counts):
    parts, at = [], 0
    for count in counts:
        parts.append(refs[at : at + count])
        at += count
    return parts, refs[at:]


def estimate_kernel(shifts, counts, has_start, x, z_lo, own, other, *refs):
    start = refs[0] if has_start else None
    parts, rest = take(refs[1:] if has_start else refs, counts)
    (out,) = rest
    rows = own.shape[0]
    width = own.shape[1] // 8
    for k, pieces in enumerate(parts):
        atoms = whole(pieces)
        span = columns(chunk_place(shifts[k], x, z_lo), width)
        for low, source in ((0, own), (rows, other)):
            term = along_atoms(source[:, span], atoms)
            if k:
                out[low : low + rows] += term
            elif has_start:
                out[low : low + rows] = start[low : low + rows] + term
            else:
                out[low : low + rows] = term


def estimate(x, z_lo, own, other, start, shifts, parts):
    rows = own.shape[0]
    features = sum(p.shape[0] for p in parts[0])
    counts = tuple(len(p) for p in parts)
    flat = [p for pieces in parts for p in pieces]
    given = [own, other] + ([] if start is None else [start]) + flat
    return pl.pallas_call(
        functools.partial(estimate_kernel, shifts, counts, start is not None),
        out_shape=pltpu.VMEM((2 * rows, features), F32),
        in_specs=[SMEM, SMEM] + [VMEM] * len(given),
        out_specs=VMEM,
        compiler_params=PARAMS,
        name="estimate",
    )(x, z_lo, *[near_memory(v) for v in given])


def misfit_of(mine, theirs, signal_own, signal_other):
    rows = signal_own.shape[0]
    first = mine[0:rows] + theirs[rows : 2 * rows] - signal_own[...].astype(F32)
    second = mine[rows : 2 * rows] + theirs[0:rows] - signal_other[...].astype(F32)
    return jnp.concatenate([first.astype(BF16), second.astype(BF16)], axis=0)


def update_kernel(shifts, counts, x, z_lo, own, other, mine, theirs, signal_own, signal_other, *refs):
    parts, rest = take(refs, counts)
    fresh_own, fresh_other, out = rest
    rows = own.shape[0]
    width = own.shape[1] // 8
    misfit = misfit_of(mine, theirs, signal_own, signal_other)
    for k, pieces in enumerate(parts):
        atoms = whole(pieces)
        span = columns(chunk_place(shifts[k], x, z_lo), width)
        for low, source, target in ((0, own, fresh_own), (rows, other, fresh_other)):
            correlation = jnp.dot(misfit[low : low + rows], atoms, preferred_element_type=F32)
            value = source[:, span].astype(F32) - 4.0 * correlation
            fresh = (value - jnp.clip(value, -0.5, 0.5)).astype(BF16)
            target[:, span] = fresh
            term = along_atoms(fresh, atoms)
            if k:
                out[low : low + rows] += term
            else:
                out[low : low + rows] = term


def update(x, z_lo, own, other, mine, theirs, signal_own, signal_other, shifts, parts):
    rows = own.shape[0]
    features = sum(p.shape[0] for p in parts[0])
    counts = tuple(len(p) for p in parts)
    flat = [p for pieces in parts for p in pieces]
    given = [own, other, mine, theirs, signal_own, signal_other] + flat
    return pl.pallas_call(
        functools.partial(update_kernel, shifts, counts),
        out_shape=(
            pltpu.VMEM(own.shape, BF16),
            pltpu.VMEM(own.shape, BF16),
            pltpu.VMEM((2 * rows, features), F32),
        ),
        in_specs=[SMEM, SMEM] + [VMEM] * len(given),
        out_specs=(VMEM,) * 3,
        compiler_params=PARAMS,
        name="update",
    )(x, z_lo, *[near_memory(v) for v in given])


def gradient_kernel(core, mine, theirs, signal_own, signal_other, own, other, out, codes_out, buf, sems, piece_sems):
    width = own.shape[1] // 8
    copies = []
    for q in range(8):
        target = codes_out.at[:, columns(2 * q + core[0], width)]
        copies.append(pltpu.make_async_copy(own.at[:, columns(q, width)], target, sems.at[q]))
    misfit = misfit_of(mine, theirs, signal_own, signal_other)
    wide = jnp.concatenate([misfit, misfit[:, 128:192]], axis=1)
    part = width // 8
    low = lax.broadcasted_iota(jnp.int32, (part // 2, 128), 1) < 64
    for q in range(8):
        span = slice(q * width, (q + 1) * width)
        codes = jnp.concatenate([own[:, span], other[:, span]], axis=0)
        product = lax.dot_general(codes, wide, (((0,), (0,)), ((), ())), preferred_element_type=F32)
        for n in range(8):
            piece = product[n * part : (n + 1) * part]
            buf[q * 8 + n, 0:part] = piece[:, 0:128].astype(BF16)
            tail = jnp.where(low, piece[: part // 2, 128:256], piece[part // 2 :, 128:256])
            buf[q * 8 + n, part : part + part // 2] = tail.astype(BF16)
        copy = pltpu.make_async_copy(buf.at[q * 8 : q * 8 + 8], out.at[q * 8 : q * 8 + 8], piece_sems.at[q])
        copy.start()
        copies.append(copy)
        copies[q].start()
    for copy in copies:
        copy.wait()


def gradient(core, mine, theirs, signal_own, signal_other, own, other):
    part = own.shape[1] // 64
    given = [mine, theirs, signal_own, signal_other, own, other]
    pieces = (64, part + part // 2, 128)
    return pl.pallas_call(
        gradient_kernel,
        out_shape=(
            pltpu.HBM(pieces, BF16),
            pltpu.HBM((own.shape[0], 2 * own.shape[1]), BF16),
        ),
        in_specs=[SMEM] + [VMEM] * 6,
        out_specs=(ANY, ANY),
        scratch_shapes=[
            pltpu.VMEM(pieces, BF16),
            pltpu.SemaphoreType.DMA((8,)),
            pltpu.SemaphoreType.DMA((8,)),
        ],
        compiler_params=PARAMS,
        name="gradient",
    )(core, *[near_memory(v) for v in given])


def place_kernel(core, fresh_back, codes, codes_out, sems):
    width = fresh_back.shape[1] // 8
    copies = []
    for q in range(8):
        target = codes_out.at[:, columns(2 * q + 1 - core[0], width)]
        copies.append(pltpu.make_async_copy(fresh_back.at[:, columns(q, width)], target, sems.at[q]))
    for copy in copies:
        copy.start()
    for copy in copies:
        copy.wait()


def place(core, fresh_back, codes):
    return pl.pallas_call(
        place_kernel,
        out_shape=pltpu.HBM(codes.shape, BF16),
        in_specs=[SMEM, VMEM, ANY],
        out_specs=ANY,
        scratch_shapes=[pltpu.SemaphoreType.DMA((8,))],
        input_output_aliases={2: 0},
        compiler_params=PARAMS,
        name="place",
    )(core, near_memory(fresh_back), far_memory(codes))


def finish_kernel(scale, pieces, grad_out):
    part = grad_out.shape[0]
    total = pieces[0].astype(F32)
    for i in range(1, pieces.shape[0]):
        total = total + pieces[i].astype(F32)
    total = total * scale
    grad_out[:, 0:128] = total[0:part]
    grad_out[0 : part // 2, 128:192] = total[part:, 0:64]
    grad_out[part // 2 :, 128:192] = total[part:, 64:128]


def finish(scale, pieces, grad_shape):
    return pl.pallas_call(
        functools.partial(finish_kernel, scale),
        out_shape=jax.ShapeDtypeStruct(grad_shape, F32),
        in_specs=[VMEM],
        out_specs=VMEM,
        compiler_params=PARAMS,
        name="finish",
    )(near_memory(pieces))


def step(codes, signals, dictionary):
    rows, atom_count = codes.shape
    core, x, z_lo = (lax.axis_index(a).astype(jnp.int32).reshape(1) for a in ("core", "x", "z_lo"))
    atoms = dictionary.T
    mid = atoms.shape[0] // 2
    left = send_x(atoms, 1)
    right = send_x(atoms, -1)
    low, high = halve(core, x, z_lo, atoms)
    near = (send_z(low, 1), send_z(high, -1))
    own, away = split(core, codes)
    other = send_core(away)
    signal_other = send_core(signals)
    far = (send_x(left[:mid], 1), send_x(right[mid:], -1))
    near_left = send_z(left, 1)
    near_right = send_z(right, -1)
    near_far = (send_z(far[0], 1), send_z(far[1], -1))
    plan = [
        ((0, 0), (low, high)),
        ((0, 3), (left,)),
        ((0, 1), (right,)),
        ((1, 0), near),
        ((0, 2), far),
        ((1, 3), (near_left,)),
        ((1, 1), (near_right,)),
        ((1, 2), near_far),
    ]
    shifts = [p[0] for p in plan]
    parts = [p[1] for p in plan]
    mine = None
    for first, last in ((0, 4), (4, 7), (7, 8)):
        mine = estimate(x, z_lo, own, other, mine, shifts[first:last], parts[first:last])
    theirs = send_core(mine)
    fresh_own, fresh_other, second = update(
        x, z_lo, own, other, mine, theirs, signals, signal_other, shifts, parts
    )
    second_theirs = send_core(second)
    fresh_back = send_core(fresh_other)
    pieces, fresh = gradient(core, second, second_theirs, signals, signal_other, fresh_own, fresh_other)
    pieces = functools.partial(lax.all_to_all, tiled=True)(pieces, ("z_lo", "x", "z_hi", "y"), 0, 0)
    fresh = place(core, fresh_back, fresh)
    total_rows = rows
    for size in SIZES:
        total_rows *= size
    grad_shape = (atom_count // 128, signals.shape[1])
    return fresh, finish(float(total_rows) ** -0.5, pieces, grad_shape)


def solution(mesh):
    fine = Mesh(mesh.devices.reshape(SIZES), AXES)
    every = P(AXES, None)
    return jax.shard_map(
        step,
        mesh=fine,
        in_specs=(every, every, P(("z_lo", "x", "core"), None)),
        out_specs=(every, every),
        check_vma=False,
    )
```

```python
import functools

import jax
import jax.numpy as jnp
from jax import lax
from jax.experimental import pallas as pl
from jax.experimental.pallas import tpu as pltpu
from jax.sharding import Mesh
from jax.sharding import PartitionSpec as P


AXES = ("z_lo", "x", "core", "z_hi", "y")
SIZES = (2, 4, 2, 2, 4)
ANY = pl.BlockSpec(memory_space=pl.ANY)
SMEM = pl.BlockSpec(memory_space=pltpu.SMEM)
VMEM = pl.BlockSpec(memory_space=pltpu.VMEM)
F32, BF16 = jnp.float32, jnp.bfloat16
PARAMS = pltpu.CompilerParams(vmem_limit_bytes=24 << 20)


def near_memory(value):
    return pltpu.with_memory_space_constraint(value, pltpu.VMEM)


def far_memory(value):
    return pltpu.with_memory_space_constraint(value, pltpu.HBM)


def z_step(step):
    def place(z):
        return (z % 2) * 2 + z // 2

    return [(place(z), place((z + step) % 4)) for z in range(4)]


def send_x(value, step):
    return lax.ppermute(value, "x", [(i, (i + step) % 4) for i in range(4)])


def send_z(value, step):
    return lax.ppermute(value, ("z_lo", "z_hi"), z_step(step))


def send_core(value):
    return lax.ppermute(value, "core", [(0, 1), (1, 0)])


def columns(block, width):
    return pl.ds(pl.multiple_of(block * width, 128), width)


def chunk_place(shift, x, z_lo):
    dz, dx = shift
    return ((z_lo[0] + dz) % 2) * 4 + (x[0] + dx) % 4


def halve_kernel(core, x, z_lo, atoms, low, high, sems):
    mid = low.shape[0]
    copies = [
        pltpu.make_async_copy(atoms.at[0:mid], low, sems.at[0]),
        pltpu.make_async_copy(atoms.at[mid : 2 * mid], high, sems.at[1]),
    ]
    for copy in copies:
        copy.start()
    for copy in copies:
        copy.wait()


def halve(core, x, z_lo, atoms):
    piece = pltpu.VMEM((atoms.shape[0] // 2, atoms.shape[1]), BF16)
    return pl.pallas_call(
        halve_kernel,
        out_shape=(piece, piece),
        in_specs=[SMEM, SMEM, SMEM, ANY],
        out_specs=(VMEM, VMEM),
        scratch_shapes=[pltpu.SemaphoreType.DMA((2,))],
        compiler_params=PARAMS,
        name="halve",
    )(core, x, z_lo, far_memory(atoms))


def take_kernel(core, codes, out, sems):
    width = out.shape[1] // 8
    copies = []
    for q in range(8):
        source = codes.at[:, columns(2 * q + core[0], width)]
        copies.append(pltpu.make_async_copy(source, out.at[:, columns(q, width)], sems.at[q]))
    for copy in copies:
        copy.start()
    for copy in copies:
        copy.wait()


def take_half(core, codes):
    rows, atom_count = codes.shape
    return pl.pallas_call(
        take_kernel,
        out_shape=pltpu.VMEM((rows, atom_count // 2), BF16),
        in_specs=[SMEM, ANY],
        out_specs=VMEM,
        scratch_shapes=[pltpu.SemaphoreType.DMA((8,))],
        compiler_params=PARAMS,
        name="take",
    )(core, far_memory(codes))


def along_atoms(left, right):
    return lax.dot_general(left, right, (((1,), (1,)), ((), ())), preferred_element_type=F32)


def whole(pieces):
    values = [piece[...] for piece in pieces]
    return values[0] if len(values) == 1 else jnp.concatenate(values, axis=0)


def take(refs, counts):
    parts, at = [], 0
    for count in counts:
        parts.append(refs[at : at + count])
        at += count
    return parts, refs[at:]


def estimate_kernel(shifts, counts, has_start, x, z_lo, own, other, *refs):
    start = refs[0] if has_start else None
    parts, rest = take(refs[1:] if has_start else refs, counts)
    (out,) = rest
    rows = own.shape[0]
    width = own.shape[1] // 8
    for k, pieces in enumerate(parts):
        atoms = whole(pieces)
        span = columns(chunk_place(shifts[k], x, z_lo), width)
        for low, source in ((0, own), (rows, other)):
            term = along_atoms(source[:, span], atoms)
            if k:
                out[low : low + rows] += term
            elif has_start:
                out[low : low + rows] = start[low : low + rows] + term
            else:
                out[low : low + rows] = term


def estimate(x, z_lo, own, other, start, shifts, parts):
    rows = own.shape[0]
    features = sum(p.shape[0] for p in parts[0])
    counts = tuple(len(p) for p in parts)
    flat = [p for pieces in parts for p in pieces]
    given = [own, other] + ([] if start is None else [start]) + flat
    return pl.pallas_call(
        functools.partial(estimate_kernel, shifts, counts, start is not None),
        out_shape=pltpu.VMEM((2 * rows, features), F32),
        in_specs=[SMEM, SMEM] + [VMEM] * len(given),
        out_specs=VMEM,
        compiler_params=PARAMS,
        name="estimate",
    )(x, z_lo, *[near_memory(v) for v in given])


def misfit_of(mine, theirs, signal_own, signal_other):
    rows = signal_own.shape[0]
    first = mine[0:rows] + theirs[rows : 2 * rows] - signal_own[...].astype(F32)
    second = mine[rows : 2 * rows] + theirs[0:rows] - signal_other[...].astype(F32)
    return jnp.concatenate([first.astype(BF16), second.astype(BF16)], axis=0)


def update_kernel(shifts, counts, core, x, z_lo, own, other, mine, theirs, signal_own, signal_other, *refs):
    parts, rest = take(refs, counts)
    fresh_own, fresh_other, out, codes_out, back, sems = rest
    copies = []
    rows = own.shape[0]
    width = own.shape[1] // 8
    misfit = misfit_of(mine, theirs, signal_own, signal_other)
    for k, pieces in enumerate(parts):
        atoms = whole(pieces)
        span = columns(chunk_place(shifts[k], x, z_lo), width)
        for low, source, target in ((0, own, fresh_own), (rows, other, fresh_other)):
            correlation = jnp.dot(misfit[low : low + rows], atoms, preferred_element_type=F32)
            value = source[:, span].astype(F32) - 4.0 * correlation
            fresh = (value - jnp.clip(value, -0.5, 0.5)).astype(BF16)
            target[:, span] = fresh
            if target is fresh_own:
                block = 2 * chunk_place(shifts[k], x, z_lo) + core[0]
                copy = pltpu.make_async_copy(target.at[:, span], codes_out.at[:, columns(block, width)], sems.at[0, k])
            else:
                copy = pltpu.make_async_copy(target.at[:, span], back.at[:, span], sems.at[1, k])
            copy.start()
            copies.append(copy)
            term = along_atoms(fresh, atoms)
            if k:
                out[low : low + rows] += term
            else:
                out[low : low + rows] = term
    for copy in copies:
        copy.wait()


def update(core, x, z_lo, own, other, mine, theirs, signal_own, signal_other, shifts, parts):
    rows = own.shape[0]
    features = sum(p.shape[0] for p in parts[0])
    counts = tuple(len(p) for p in parts)
    flat = [p for pieces in parts for p in pieces]
    given = [own, other, mine, theirs, signal_own, signal_other] + flat
    return pl.pallas_call(
        functools.partial(update_kernel, shifts, counts),
        out_shape=(
            pltpu.VMEM(own.shape, BF16),
            pltpu.VMEM(own.shape, BF16),
            pltpu.VMEM((2 * rows, features), F32),
            pltpu.HBM((rows, 2 * own.shape[1]), BF16),
            pltpu.HBM(own.shape, BF16),
        ),
        in_specs=[SMEM] * 3 + [VMEM] * len(given),
        out_specs=(VMEM,) * 3 + (ANY, ANY),
        scratch_shapes=[pltpu.SemaphoreType.DMA((2, len(parts)))],
        compiler_params=PARAMS,
        name="update",
    )(core, x, z_lo, *[near_memory(v) for v in given])


def gradient_kernel(mine, theirs, signal_own, signal_other, own, other, out, buf, sems):
    width = own.shape[1] // 8
    copies = []
    misfit = misfit_of(mine, theirs, signal_own, signal_other)
    wide = jnp.concatenate([misfit, misfit[:, 128:192]], axis=1)
    part = width // 8
    low = lax.broadcasted_iota(jnp.int32, (part // 2, 128), 1) < 64
    for q in range(8):
        span = slice(q * width, (q + 1) * width)
        codes = jnp.concatenate([own[:, span], other[:, span]], axis=0)
        product = lax.dot_general(codes, wide, (((0,), (0,)), ((), ())), preferred_element_type=F32)
        for n in range(8):
            piece = product[n * part : (n + 1) * part]
            buf[q * 8 + n, 0:part] = piece[:, 0:128].astype(BF16)
            tail = jnp.where(low, piece[: part // 2, 128:256], piece[part // 2 :, 128:256])
            buf[q * 8 + n, part : part + part // 2] = tail.astype(BF16)
        copy = pltpu.make_async_copy(buf.at[q * 8 : q * 8 + 8], out.at[q * 8 : q * 8 + 8], sems.at[q])
        copy.start()
        copies.append(copy)
    for copy in copies:
        copy.wait()


def gradient(mine, theirs, signal_own, signal_other, own, other):
    part = own.shape[1] // 64
    given = [mine, theirs, signal_own, signal_other, own, other]
    pieces = (64, part + part // 2, 128)
    return pl.pallas_call(
        gradient_kernel,
        out_shape=pltpu.HBM(pieces, BF16),
        in_specs=[VMEM] * 6,
        out_specs=ANY,
        scratch_shapes=[pltpu.VMEM(pieces, BF16), pltpu.SemaphoreType.DMA((8,))],
        compiler_params=PARAMS,
        name="gradient",
    )(*[near_memory(v) for v in given])


def place_kernel(core, fresh_back, codes, codes_out, sems):
    width = fresh_back.shape[1] // 8
    copies = []
    for q in range(8):
        target = codes_out.at[:, columns(2 * q + 1 - core[0], width)]
        copies.append(pltpu.make_async_copy(fresh_back.at[:, columns(q, width)], target, sems.at[q]))
    for copy in copies:
        copy.start()
    for copy in copies:
        copy.wait()


def place(core, fresh_back, codes):
    return pl.pallas_call(
        place_kernel,
        out_shape=pltpu.HBM(codes.shape, BF16),
        in_specs=[SMEM, VMEM, ANY],
        out_specs=ANY,
        scratch_shapes=[pltpu.SemaphoreType.DMA((8,))],
        input_output_aliases={2: 0},
        compiler_params=PARAMS,
        name="place",
    )(core, near_memory(fresh_back), far_memory(codes))


def finish_kernel(scale, pieces, grad_out):
    part = grad_out.shape[0]
    total = pieces[0].astype(F32)
    for i in range(1, pieces.shape[0]):
        total = total + pieces[i].astype(F32)
    total = total * scale
    grad_out[:, 0:128] = total[0:part]
    grad_out[0 : part // 2, 128:192] = total[part:, 0:64]
    grad_out[part // 2 :, 128:192] = total[part:, 64:128]


def finish(scale, pieces, grad_shape):
    return pl.pallas_call(
        functools.partial(finish_kernel, scale),
        out_shape=jax.ShapeDtypeStruct(grad_shape, F32),
        in_specs=[VMEM],
        out_specs=VMEM,
        compiler_params=PARAMS,
        name="finish",
    )(near_memory(pieces))


def step(codes, signals, dictionary):
    rows, atom_count = codes.shape
    core, x, z_lo = (lax.axis_index(a).astype(jnp.int32).reshape(1) for a in ("core", "x", "z_lo"))
    atoms = dictionary.T
    mid = atoms.shape[0] // 2
    left = send_x(atoms, 1)
    right = send_x(atoms, -1)
    low, high = halve(core, x, z_lo, atoms)
    near = (send_z(low, 1), send_z(high, -1))
    away = take_half(1 - core, codes)
    other = send_core(away)
    own = take_half(core, codes)
    signal_other = send_core(signals)
    far = (send_x(left[:mid], 1), send_x(right[mid:], -1))
    near_left = send_z(left, 1)
    near_right = send_z(right, -1)
    near_far = (send_z(far[0], 1), send_z(far[1], -1))
    plan = [
        ((0, 0), (low, high)),
        ((0, 3), (left,)),
        ((0, 1), (right,)),
        ((1, 0), near),
        ((0, 2), far),
        ((1, 3), (near_left,)),
        ((1, 1), (near_right,)),
        ((1, 2), near_far),
    ]
    shifts = [p[0] for p in plan]
    parts = [p[1] for p in plan]
    mine = None
    for first, last in ((0, 4), (4, 7), (7, 8)):
        mine = estimate(x, z_lo, own, other, mine, shifts[first:last], parts[first:last])
    theirs = send_core(mine)
    fresh_own, fresh_other, second, fresh, back = update(
        core, x, z_lo, own, other, mine, theirs, signals, signal_other, shifts, parts
    )
    second_theirs = send_core(second)
    fresh_back = send_core(back)
    pieces = gradient(second, second_theirs, signals, signal_other, fresh_own, fresh_other)
    pieces = functools.partial(lax.all_to_all, tiled=True)(pieces, ("z_lo", "x", "z_hi", "y"), 0, 0)
    fresh = place(core, fresh_back, fresh)
    total_rows = rows
    for size in SIZES:
        total_rows *= size
    grad_shape = (atom_count // 128, signals.shape[1])
    return fresh, finish(float(total_rows) ** -0.5, pieces, grad_shape)


def solution(mesh):
    fine = Mesh(mesh.devices.reshape(SIZES), AXES)
    every = P(AXES, None)
    return jax.shard_map(
        step,
        mesh=fine,
        in_specs=(every, every, P(("z_lo", "x", "core"), None)),
        out_specs=(every, every),
        check_vma=False,
    )
```

```python
import functools

import jax
import jax.numpy as jnp
from jax import lax
from jax.experimental import pallas as pl
from jax.experimental.pallas import tpu as pltpu
from jax.sharding import Mesh
from jax.sharding import PartitionSpec as P


AXES = ("z_lo", "x", "core", "z_hi", "y")
SIZES = (2, 4, 2, 2, 4)
ANY = pl.BlockSpec(memory_space=pl.ANY)
SMEM = pl.BlockSpec(memory_space=pltpu.SMEM)
VMEM = pl.BlockSpec(memory_space=pltpu.VMEM)
F32, BF16 = jnp.float32, jnp.bfloat16
PARAMS = pltpu.CompilerParams(vmem_limit_bytes=24 << 20)


def near_memory(value):
    return pltpu.with_memory_space_constraint(value, pltpu.VMEM)


def far_memory(value):
    return pltpu.with_memory_space_constraint(value, pltpu.HBM)


def send(value, dx, dz):
    def index(z, x, c):
        return (((z % 2) * 4 + x) * 2 + c) * 2 + z // 2

    pairs = []
    for z in range(4):
        for x in range(4):
            for c, way in ((0, 1), (1, -1)):
                pairs.append((index(z, x, c), index((z + way * dz) % 4, (x + way * dx) % 4, c)))
    return lax.ppermute(value, ("z_lo", "x", "core", "z_hi"), pairs)


def send_core(value):
    return lax.ppermute(value, "core", [(0, 1), (1, 0)])


def columns(block, width):
    return pl.ds(pl.multiple_of(block * width, 128), width)


def chunk_place(shift, core, x, z_lo):
    dz, dx = shift
    return ((z_lo[0] + dz) % 2) * 4 + (x[0] + 4 + dx * (1 - 2 * core[0])) % 4


def take_kernel(flip, core, x, z_lo, codes, out, sems):
    width = out.shape[1] // 8
    half = 1 - core[0] if flip else core[0]
    copies = []
    for q in range(8):
        source = codes.at[:, columns(2 * q + half, width)]
        copies.append(pltpu.make_async_copy(source, out.at[:, columns(q, width)], sems.at[q]))
    for copy in copies:
        copy.start()
    for copy in copies:
        copy.wait()


def take_half(flip, core, x, z_lo, codes):
    rows, atom_count = codes.shape
    return pl.pallas_call(
        functools.partial(take_kernel, flip),
        out_shape=pltpu.VMEM((rows, atom_count // 2), BF16),
        in_specs=[SMEM, SMEM, SMEM, ANY],
        out_specs=VMEM,
        scratch_shapes=[pltpu.SemaphoreType.DMA((8,))],
        compiler_params=PARAMS,
        name="take",
    )(core, x, z_lo, far_memory(codes))


def along_atoms(left, right):
    return lax.dot_general(left, right, (((1,), (1,)), ((), ())), preferred_element_type=F32)


def whole(pieces):
    values = [piece[...] for piece in pieces]
    return values[0] if len(values) == 1 else jnp.concatenate(values, axis=0)


def take(refs, counts):
    parts, at = [], 0
    for count in counts:
        parts.append(refs[at : at + count])
        at += count
    return parts, refs[at:]


def estimate_kernel(shifts, counts, has_start, core, x, z_lo, own, other, *refs):
    start = refs[0] if has_start else None
    parts, rest = take(refs[1:] if has_start else refs, counts)
    (out,) = rest
    rows = own.shape[0]
    width = own.shape[1] // 8
    for k, pieces in enumerate(parts):
        atoms = whole(pieces)
        span = columns(chunk_place(shifts[k], core, x, z_lo), width)
        for low, source in ((0, own), (rows, other)):
            term = along_atoms(source[:, span], atoms)
            if k:
                out[low : low + rows] += term
            elif has_start:
                out[low : low + rows] = start[low : low + rows] + term
            else:
                out[low : low + rows] = term


def estimate(core, x, z_lo, own, other, start, shifts, parts):
    rows = own.shape[0]
    features = sum(p.shape[0] for p in parts[0])
    counts = tuple(len(p) for p in parts)
    flat = [p for pieces in parts for p in pieces]
    given = [own, other] + ([] if start is None else [start]) + flat
    return pl.pallas_call(
        functools.partial(estimate_kernel, shifts, counts, start is not None),
        out_shape=pltpu.VMEM((2 * rows, features), F32),
        in_specs=[SMEM] * 3 + [VMEM] * len(given),
        out_specs=VMEM,
        compiler_params=PARAMS,
        name="estimate",
    )(core, x, z_lo, *[near_memory(v) for v in given])


def misfit_of(mine, theirs, signal_own, signal_other):
    rows = signal_own.shape[0]
    first = mine[0:rows] + theirs[rows : 2 * rows] - signal_own[...].astype(F32)
    second = mine[rows : 2 * rows] + theirs[0:rows] - signal_other[...].astype(F32)
    return jnp.concatenate([first.astype(BF16), second.astype(BF16)], axis=0)


def update_kernel(shifts, counts, core, x, z_lo, own, other, mine, theirs, signal_own, signal_other, *refs):
    parts, rest = take(refs, counts)
    fresh_own, fresh_other, out, codes_out, back, sems = rest
    copies = []
    rows = own.shape[0]
    width = own.shape[1] // 8
    misfit = misfit_of(mine, theirs, signal_own, signal_other)
    for k, pieces in enumerate(parts):
        atoms = whole(pieces)
        span = columns(chunk_place(shifts[k], core, x, z_lo), width)
        for low, source, target in ((0, own, fresh_own), (rows, other, fresh_other)):
            correlation = jnp.dot(misfit[low : low + rows], atoms, preferred_element_type=F32)
            value = source[:, span].astype(F32) - 4.0 * correlation
            fresh = (value - jnp.clip(value, -0.5, 0.5)).astype(BF16)
            target[:, span] = fresh
            if target is fresh_own:
                block = 2 * chunk_place(shifts[k], core, x, z_lo) + core[0]
                copy = pltpu.make_async_copy(target.at[:, span], codes_out.at[:, columns(block, width)], sems.at[0, k])
            else:
                copy = pltpu.make_async_copy(target.at[:, span], back.at[:, span], sems.at[1, k])
            copy.start()
            copies.append(copy)
            term = along_atoms(fresh, atoms)
            if k:
                out[low : low + rows] += term
            else:
                out[low : low + rows] = term
    for copy in copies:
        copy.wait()


def update(core, x, z_lo, own, other, mine, theirs, signal_own, signal_other, shifts, parts):
    rows = own.shape[0]
    features = sum(p.shape[0] for p in parts[0])
    counts = tuple(len(p) for p in parts)
    flat = [p for pieces in parts for p in pieces]
    given = [own, other, mine, theirs, signal_own, signal_other] + flat
    return pl.pallas_call(
        functools.partial(update_kernel, shifts, counts),
        out_shape=(
            pltpu.VMEM(own.shape, BF16),
            pltpu.VMEM(own.shape, BF16),
            pltpu.VMEM((2 * rows, features), F32),
            pltpu.HBM((rows, 2 * own.shape[1]), BF16),
            pltpu.HBM(own.shape, BF16),
        ),
        in_specs=[SMEM] * 3 + [VMEM] * len(given),
        out_specs=(VMEM,) * 3 + (ANY, ANY),
        scratch_shapes=[pltpu.SemaphoreType.DMA((2, len(parts)))],
        compiler_params=PARAMS,
        name="update",
    )(core, x, z_lo, *[near_memory(v) for v in given])


def gradient_kernel(mine, theirs, signal_own, signal_other, own, other, out, buf, sems):
    width = own.shape[1] // 8
    copies = []
    misfit = misfit_of(mine, theirs, signal_own, signal_other)
    wide = jnp.concatenate([misfit, misfit[:, 128:192]], axis=1)
    part = width // 8
    low = lax.broadcasted_iota(jnp.int32, (part // 2, 128), 1) < 64
    for q in range(8):
        span = slice(q * width, (q + 1) * width)
        codes = jnp.concatenate([own[:, span], other[:, span]], axis=0)
        product = lax.dot_general(codes, wide, (((0,), (0,)), ((), ())), preferred_element_type=F32)
        for n in range(8):
            piece = product[n * part : (n + 1) * part]
            buf[q * 8 + n, 0:part] = piece[:, 0:128].astype(BF16)
            tail = jnp.where(low, piece[: part // 2, 128:256], piece[part // 2 :, 128:256])
            buf[q * 8 + n, part : part + part // 2] = tail.astype(BF16)
        copy = pltpu.make_async_copy(buf.at[q * 8 : q * 8 + 8], out.at[q * 8 : q * 8 + 8], sems.at[q])
        copy.start()
        copies.append(copy)
    for copy in copies:
        copy.wait()


def gradient(mine, theirs, signal_own, signal_other, own, other):
    part = own.shape[1] // 64
    given = [mine, theirs, signal_own, signal_other, own, other]
    pieces = (64, part + part // 2, 128)
    return pl.pallas_call(
        gradient_kernel,
        out_shape=pltpu.HBM(pieces, BF16),
        in_specs=[VMEM] * 6,
        out_specs=ANY,
        scratch_shapes=[pltpu.VMEM(pieces, BF16), pltpu.SemaphoreType.DMA((8,))],
        compiler_params=PARAMS,
        name="gradient",
    )(*[near_memory(v) for v in given])


def place_kernel(core, fresh_back, codes, codes_out, sems):
    width = fresh_back.shape[1] // 8
    copies = []
    for q in range(8):
        target = codes_out.at[:, columns(2 * q + 1 - core[0], width)]
        copies.append(pltpu.make_async_copy(fresh_back.at[:, columns(q, width)], target, sems.at[q]))
    for copy in copies:
        copy.start()
    for copy in copies:
        copy.wait()


def place(core, fresh_back, codes):
    return pl.pallas_call(
        place_kernel,
        out_shape=pltpu.HBM(codes.shape, BF16),
        in_specs=[SMEM, VMEM, ANY],
        out_specs=ANY,
        scratch_shapes=[pltpu.SemaphoreType.DMA((8,))],
        input_output_aliases={2: 0},
        compiler_params=PARAMS,
        name="place",
    )(core, near_memory(fresh_back), far_memory(codes))


def finish_kernel(scale, pieces, grad_out):
    part = grad_out.shape[0]
    total = pieces[0].astype(F32)
    for i in range(1, pieces.shape[0]):
        total = total + pieces[i].astype(F32)
    total = total * scale
    grad_out[:, 0:128] = total[0:part]
    grad_out[0 : part // 2, 128:192] = total[part:, 0:64]
    grad_out[part // 2 :, 128:192] = total[part:, 64:128]


def finish(scale, pieces, grad_shape):
    return pl.pallas_call(
        functools.partial(finish_kernel, scale),
        out_shape=jax.ShapeDtypeStruct(grad_shape, F32),
        in_specs=[VMEM],
        out_specs=VMEM,
        compiler_params=PARAMS,
        name="finish",
    )(near_memory(pieces))


def step(codes, signals, dictionary):
    rows, atom_count = codes.shape
    core, x, z_lo = (lax.axis_index(a).astype(jnp.int32).reshape(1) for a in ("core", "x", "z_lo"))
    atoms = dictionary.T
    side = send(atoms, 1, 0)
    near = send(atoms, 0, 1)
    reverse = send(atoms, -1, 0)
    away = take_half(True, core, x, z_lo, codes)
    other = send_core(away)
    own = take_half(False, core, x, z_lo, codes)
    signal_other = send_core(signals)
    far = send(side, 1, 0)
    near_far = send(side, 1, 1)
    near_side = send(atoms, 1, 1)
    near_reverse = send(reverse, 0, 1)
    plan = [
        ((0, 0), (atoms,)),
        ((0, -1), (side,)),
        ((0, 1), (reverse,)),
        ((1, 0), (near,)),
        ((0, 2), (far,)),
        ((1, 2), (near_far,)),
        ((1, -1), (near_side,)),
        ((1, 1), (near_reverse,)),
    ]
    shifts = [p[0] for p in plan]
    parts = [p[1] for p in plan]
    mine = None
    for first, last in ((0, 4), (4, 7), (7, 8)):
        mine = estimate(core, x, z_lo, own, other, mine, shifts[first:last], parts[first:last])
    theirs = send_core(mine)
    fresh_own, fresh_other, second, fresh, back = update(
        core, x, z_lo, own, other, mine, theirs, signals, signal_other, shifts, parts
    )
    second_theirs = send_core(second)
    fresh_back = send_core(back)
    pieces = gradient(second, second_theirs, signals, signal_other, fresh_own, fresh_other)
    pieces = functools.partial(lax.all_to_all, tiled=True)(pieces, ("z_lo", "x", "z_hi", "y"), 0, 0)
    fresh = place(core, fresh_back, fresh)
    total_rows = rows
    for size in SIZES:
        total_rows *= size
    grad_shape = (atom_count // 128, signals.shape[1])
    return fresh, finish(float(total_rows) ** -0.5, pieces, grad_shape)


def solution(mesh):
    fine = Mesh(mesh.devices.reshape(SIZES), AXES)
    every = P(AXES, None)
    return jax.shard_map(
        step,
        mesh=fine,
        in_specs=(every, every, P(("z_lo", "x", "core"), None)),
        out_specs=(every, every),
        check_vma=False,
    )
```

```python
import functools

import jax
import jax.numpy as jnp
from jax import lax
from jax.experimental import pallas as pl
from jax.experimental.pallas import tpu as pltpu
from jax.sharding import Mesh
from jax.sharding import PartitionSpec as P


AXES = ("z_lo", "x", "core", "z_hi", "y")
SIZES = (2, 4, 2, 2, 4)
ANY = pl.BlockSpec(memory_space=pl.ANY)
SMEM = pl.BlockSpec(memory_space=pltpu.SMEM)
VMEM = pl.BlockSpec(memory_space=pltpu.VMEM)
F32, BF16 = jnp.float32, jnp.bfloat16
PARAMS = pltpu.CompilerParams(vmem_limit_bytes=24 << 20)


def near_memory(value):
    return pltpu.with_memory_space_constraint(value, pltpu.VMEM)


def far_memory(value):
    return pltpu.with_memory_space_constraint(value, pltpu.HBM)


def send(value, dx, dz):
    def index(z, x, c):
        return (((z % 2) * 4 + x) * 2 + c) * 2 + z // 2

    pairs = []
    for z in range(4):
        for x in range(4):
            for c, way in ((0, 1), (1, -1)):
                pairs.append((index(z, x, c), index((z + way * dz) % 4, (x + way * dx) % 4, c)))
    return lax.ppermute(value, ("z_lo", "x", "core", "z_hi"), pairs)


def send_core(value):
    return lax.ppermute(value, "core", [(0, 1), (1, 0)])


def columns(block, width):
    return pl.ds(pl.multiple_of(block * width, 128), width)


def chunk_place(shift, core, x, z_lo):
    dz, dx = shift
    return ((z_lo[0] + dz) % 2) * 4 + (x[0] + 4 + dx * (1 - 2 * core[0])) % 4


def take_kernel(flip, core, x, z_lo, codes, out, sems):
    width = out.shape[1] // 8
    half = 1 - core[0] if flip else core[0]
    copies = []
    for q in range(8):
        source = codes.at[:, columns(2 * q + half, width)]
        copies.append(pltpu.make_async_copy(source, out.at[:, columns(q, width)], sems.at[q]))
    for copy in copies:
        copy.start()
    for copy in copies:
        copy.wait()


def take_half(flip, core, x, z_lo, codes):
    rows, atom_count = codes.shape
    return pl.pallas_call(
        functools.partial(take_kernel, flip),
        out_shape=pltpu.VMEM((rows, atom_count // 2), BF16),
        in_specs=[SMEM, SMEM, SMEM, ANY],
        out_specs=VMEM,
        scratch_shapes=[pltpu.SemaphoreType.DMA((8,))],
        compiler_params=PARAMS,
        name="take",
    )(core, x, z_lo, far_memory(codes))


def along_atoms(left, right):
    return lax.dot_general(left, right, (((1,), (1,)), ((), ())), preferred_element_type=F32)


def whole(pieces):
    values = [piece[...] for piece in pieces]
    return values[0] if len(values) == 1 else jnp.concatenate(values, axis=0)


def take(refs, counts):
    parts, at = [], 0
    for count in counts:
        parts.append(refs[at : at + count])
        at += count
    return parts, refs[at:]


def estimate_kernel(shifts, counts, has_start, core, x, z_lo, own, other, *refs):
    start = refs[0] if has_start else None
    parts, rest = take(refs[1:] if has_start else refs, counts)
    (out,) = rest
    rows = own.shape[0]
    width = own.shape[1] // 8
    for k, pieces in enumerate(parts):
        atoms = whole(pieces)
        span = columns(chunk_place(shifts[k], core, x, z_lo), width)
        for low, source in ((0, own), (rows, other)):
            term = along_atoms(source[:, span], atoms)
            if k:
                out[low : low + rows] += term
            elif has_start:
                out[low : low + rows] = start[low : low + rows] + term
            else:
                out[low : low + rows] = term


def estimate(core, x, z_lo, own, other, start, shifts, parts):
    rows = own.shape[0]
    features = sum(p.shape[0] for p in parts[0])
    counts = tuple(len(p) for p in parts)
    flat = [p for pieces in parts for p in pieces]
    given = [own, other] + ([] if start is None else [start]) + flat
    return pl.pallas_call(
        functools.partial(estimate_kernel, shifts, counts, start is not None),
        out_shape=pltpu.VMEM((2 * rows, features), F32),
        in_specs=[SMEM] * 3 + [VMEM] * len(given),
        out_specs=VMEM,
        compiler_params=PARAMS,
        name="estimate",
    )(core, x, z_lo, *[near_memory(v) for v in given])


def misfit_of(mine, theirs, signal_own, signal_other):
    rows = signal_own.shape[0]
    first = mine[0:rows] + theirs[rows : 2 * rows] - signal_own[...].astype(F32)
    second = mine[rows : 2 * rows] + theirs[0:rows] - signal_other[...].astype(F32)
    return jnp.concatenate([first.astype(BF16), second.astype(BF16)], axis=0)


def update_kernel(shifts, counts, core, x, z_lo, own, other, mine, theirs, signal_own, signal_other, *refs):
    parts, rest = take(refs, counts)
    fresh_own, fresh_other, out, codes_out, back, sems = rest
    copies = []
    rows = own.shape[0]
    width = own.shape[1] // 8
    misfit = misfit_of(mine, theirs, signal_own, signal_other)
    for k, pieces in enumerate(parts):
        atoms = whole(pieces)
        span = columns(chunk_place(shifts[k], core, x, z_lo), width)
        for low, source, target in ((0, own, fresh_own), (rows, other, fresh_other)):
            correlation = jnp.dot(misfit[low : low + rows], atoms, preferred_element_type=F32)
            value = source[:, span].astype(F32) - 4.0 * correlation
            fresh = (value - jnp.clip(value, -0.5, 0.5)).astype(BF16)
            target[:, span] = fresh
            if target is fresh_own:
                block = 2 * chunk_place(shifts[k], core, x, z_lo) + core[0]
                copy = pltpu.make_async_copy(target.at[:, span], codes_out.at[:, columns(block, width)], sems.at[0, k])
            else:
                copy = pltpu.make_async_copy(target.at[:, span], back.at[:, span], sems.at[1, k])
            copy.start()
            copies.append(copy)
            term = along_atoms(fresh, atoms)
            if k:
                out[low : low + rows] += term
            else:
                out[low : low + rows] = term
    for copy in copies:
        copy.wait()


def update(core, x, z_lo, own, other, mine, theirs, signal_own, signal_other, shifts, parts):
    rows = own.shape[0]
    features = sum(p.shape[0] for p in parts[0])
    counts = tuple(len(p) for p in parts)
    flat = [p for pieces in parts for p in pieces]
    given = [own, other, mine, theirs, signal_own, signal_other] + flat
    return pl.pallas_call(
        functools.partial(update_kernel, shifts, counts),
        out_shape=(
            pltpu.VMEM(own.shape, BF16),
            pltpu.VMEM(own.shape, BF16),
            pltpu.VMEM((2 * rows, features), F32),
            pltpu.HBM((rows, 2 * own.shape[1]), BF16),
            pltpu.HBM(own.shape, BF16),
        ),
        in_specs=[SMEM] * 3 + [VMEM] * len(given),
        out_specs=(VMEM,) * 3 + (ANY, ANY),
        scratch_shapes=[pltpu.SemaphoreType.DMA((2, len(parts)))],
        compiler_params=PARAMS,
        name="update",
    )(core, x, z_lo, *[near_memory(v) for v in given])


def gradient_kernel(mine, theirs, signal_own, signal_other, own, other, out, buf, sems):
    width = own.shape[1] // 8
    copies = []
    misfit = misfit_of(mine, theirs, signal_own, signal_other)
    wide = jnp.concatenate([misfit, misfit[:, 128:192]], axis=1)
    part = width // 8
    low = lax.broadcasted_iota(jnp.int32, (part // 2, 128), 1) < 64
    for q in range(8):
        span = slice(q * width, (q + 1) * width)
        codes = jnp.concatenate([own[:, span], other[:, span]], axis=0)
        product = lax.dot_general(codes, wide, (((0,), (0,)), ((), ())), preferred_element_type=F32)
        for n in range(8):
            piece = product[n * part : (n + 1) * part]
            buf[q * 8 + n, 0:part] = piece[:, 0:128].astype(BF16)
            tail = jnp.where(low, piece[: part // 2, 128:256], piece[part // 2 :, 128:256])
            buf[q * 8 + n, part : part + part // 2] = tail.astype(BF16)
            if n % 4 == 3:
                span = slice(q * 8 + n - 3, q * 8 + n + 1)
                copy = pltpu.make_async_copy(buf.at[span], out.at[span], sems.at[q, n // 4])
                copy.start()
                copies.append(copy)
    for copy in copies:
        copy.wait()


def gradient(mine, theirs, signal_own, signal_other, own, other):
    part = own.shape[1] // 64
    given = [mine, theirs, signal_own, signal_other, own, other]
    pieces = (64, part + part // 2, 128)
    return pl.pallas_call(
        gradient_kernel,
        out_shape=pltpu.HBM(pieces, BF16),
        in_specs=[VMEM] * 6,
        out_specs=ANY,
        scratch_shapes=[pltpu.VMEM(pieces, BF16), pltpu.SemaphoreType.DMA((8, 2))],
        compiler_params=PARAMS,
        name="gradient",
    )(*[near_memory(v) for v in given])


def place_kernel(core, fresh_back, codes, codes_out, sems):
    width = fresh_back.shape[1] // 8
    copies = []
    for q in range(8):
        target = codes_out.at[:, columns(2 * q + 1 - core[0], width)]
        copies.append(pltpu.make_async_copy(fresh_back.at[:, columns(q, width)], target, sems.at[q]))
    for copy in copies:
        copy.start()
    for copy in copies:
        copy.wait()


def place(core, fresh_back, codes):
    return pl.pallas_call(
        place_kernel,
        out_shape=pltpu.HBM(codes.shape, BF16),
        in_specs=[SMEM, VMEM, ANY],
        out_specs=ANY,
        scratch_shapes=[pltpu.SemaphoreType.DMA((8,))],
        input_output_aliases={2: 0},
        compiler_params=PARAMS,
        name="place",
    )(core, near_memory(fresh_back), far_memory(codes))


def finish_kernel(scale, pieces, grad_out):
    part = grad_out.shape[0]
    total = pieces[0].astype(F32)
    for i in range(1, pieces.shape[0]):
        total = total + pieces[i].astype(F32)
    total = total * scale
    grad_out[:, 0:128] = total[0:part]
    grad_out[0 : part // 2, 128:192] = total[part:, 0:64]
    grad_out[part // 2 :, 128:192] = total[part:, 64:128]


def finish(scale, pieces, grad_shape):
    return pl.pallas_call(
        functools.partial(finish_kernel, scale),
        out_shape=jax.ShapeDtypeStruct(grad_shape, F32),
        in_specs=[VMEM],
        out_specs=VMEM,
        compiler_params=PARAMS,
        name="finish",
    )(near_memory(pieces))


def step(codes, signals, dictionary):
    rows, atom_count = codes.shape
    core, x, z_lo = (lax.axis_index(a).astype(jnp.int32).reshape(1) for a in ("core", "x", "z_lo"))
    atoms = dictionary.T
    side = send(atoms, 1, 0)
    near = send(atoms, 0, 1)
    reverse = send(atoms, -1, 0)
    away = take_half(True, core, x, z_lo, codes)
    other = send_core(away)
    own = take_half(False, core, x, z_lo, codes)
    signal_other = send_core(signals)
    far = send(side, 1, 0)
    near_far = send(side, 1, 1)
    near_side = send(atoms, 1, 1)
    near_reverse = send(reverse, 0, 1)
    plan = [
        ((0, 0), (atoms,)),
        ((0, -1), (side,)),
        ((0, 1), (reverse,)),
        ((1, 0), (near,)),
        ((0, 2), (far,)),
        ((1, 2), (near_far,)),
        ((1, -1), (near_side,)),
        ((1, 1), (near_reverse,)),
    ]
    shifts = [p[0] for p in plan]
    parts = [p[1] for p in plan]
    mine = None
    for first, last in ((0, 4), (4, 7), (7, 8)):
        mine = estimate(core, x, z_lo, own, other, mine, shifts[first:last], parts[first:last])
    theirs = send_core(mine)
    fresh_own, fresh_other, second, fresh, back = update(
        core, x, z_lo, own, other, mine, theirs, signals, signal_other, shifts, parts
    )
    second_theirs = send_core(second)
    fresh_back = send_core(back)
    pieces = gradient(second, second_theirs, signals, signal_other, fresh_own, fresh_other)
    pieces = functools.partial(lax.all_to_all, tiled=True)(pieces, ("z_lo", "x", "z_hi", "y"), 0, 0)
    fresh = place(core, fresh_back, fresh)
    total_rows = rows
    for size in SIZES:
        total_rows *= size
    grad_shape = (atom_count // 128, signals.shape[1])
    return fresh, finish(float(total_rows) ** -0.5, pieces, grad_shape)


def solution(mesh):
    fine = Mesh(mesh.devices.reshape(SIZES), AXES)
    every = P(AXES, None)
    return jax.shard_map(
        step,
        mesh=fine,
        in_specs=(every, every, P(("z_lo", "x", "core"), None)),
        out_specs=(every, every),
        check_vma=False,
    )
```
